32 devices in a mesh: tok: 4 (over z), hid: 8 (over y, x, core).
Axes of the slice: x: 2, y: 2, z: 4, core: 2. Of those that a mesh axis runs over, the one named last changes fastest.
Arguments:
- tokens: bfloat16 [2048, 1024], P('tok', 'hid'), may hold values from -6 to 6
- cotangent: bfloat16 [2048, 1024], P('tok', 'hid'), may hold values from -6 to 6
- frozen_in: bfloat16 [1024, 16384], P('tok', 'hid'), may hold values from -0.1875 to 0.1875
- frozen_out: bfloat16 [16384, 1024], P('hid', 'tok'), may hold values from -0.046875 to 0.046875
- input_adapter_first: bfloat16 [1024, 128], P('hid'), may hold values from -0.1875 to 0.1875
- input_adapter_second: bfloat16 [128, 16384], P(None, 'hid'), may hold values from -0.5 to 0.5
- adapter_out_a: bfloat16 [16384, 128], P('hid'), may hold values from -0.046875 to 0.046875
- adapter_out_b: bfloat16 [128, 1024], replicated, may hold values from -0.5 to 0.5
Outputs:
- input_gradient: float32 [2048, 1024], P('tok', 'hid')
- grad_in_a: float32 [1024, 128], P('hid')
- grad_in_b: float32 [128, 16384], P(None, 'hid')
- grad_out_a: float32 [16384, 128], P('hid')
- grad_out_b: float32 [128, 1024], P(None, 'hid')
The draws below stay inside these ranges and needn't reach their ends.
All inputs are finite; a program needn't handle non-finite values.
Results may differ from the reference program's by a relative error of at most 0.0029.
Values may be sent and summed in bfloat16 or wider, within the bound.
A program may use at most 64 MiB of HBM per device.

```python
import math
import jax
import jax.numpy as jnp
from jax import lax

D = 1024
FF = 16384
RANK = 128
TOKEN_COUNT = 2048
N_HID = 8


def levels(stream_key, extent, cuts, least, high):
    def one(axis_at, blocks):
        draws = jax.random.uniform(jax.random.fold_in(jax.random.fold_in(stream_key, 6), axis_at), (blocks,), jnp.float32, least / len(cuts), high / len(cuts))
        return jnp.repeat(jnp.exp(draws), extent[axis_at] // blocks).reshape((-1,) + (1,) * (len(extent) - axis_at - 1))

    factor_of = one(*cuts[0])
    for cut in cuts[1:]:
        factor_of = factor_of * one(*cut)
    return factor_of


def bell_draw(rng, shape, width, limit, cuts=(), kind=jnp.bfloat16):
    drawn = jax.random.normal(rng, shape, jnp.float32) * width
    if len(cuts) > 0:
        drawn = levels(rng, shape, cuts, -0.22, 0.18) * drawn
    return jnp.clip(drawn, min=-limit, max=limit).astype(kind)


def setup_inputs(seed: int = 0) -> dict:
    streams_of = jax.random.split(jax.random.key(seed), 9)
    tokens = bell_draw(streams_of[0], (TOKEN_COUNT, D), 1.0, 6.0, ((0, 4), (1, 8)))
    cotangent = bell_draw(streams_of[1], (TOKEN_COUNT, D), 1.0, 6.0, ((0, 4), (1, 8)))
    frozen_in = bell_draw(streams_of[2], (D, FF), D ** -0.5, 0.1875, ((0, 4), (1, 8)))
    frozen_out = bell_draw(streams_of[3], (FF, D), FF ** -0.5, 0.046875, ((0, 8), (1, 4)))
    input_adapter_first = bell_draw(streams_of[4], (D, RANK), D ** -0.5, 0.1875, ((0, 8),))
    input_adapter_second = bell_draw(streams_of[5], (RANK, FF), RANK ** -0.5, 0.5, ((1, 8),))
    adapter_out_a = bell_draw(streams_of[6], (FF, RANK), FF ** -0.5, 0.046875, ((0, 8),))
    adapter_out_b = bell_draw(streams_of[7], (RANK, D), RANK ** -0.5, 0.5)
    return dict(tokens=tokens, cotangent=cotangent, frozen_in=frozen_in, frozen_out=frozen_out, input_adapter_first=input_adapter_first, input_adapter_second=input_adapter_second, adapter_out_a=adapter_out_a, adapter_out_b=adapter_out_b)


ADAPTER_SCALE = 0.5
GELU_K = 0.7978845608
GELU_C = 0.044715

def gelu_pair(pre_activation):
    tangent = jnp.tanh(GELU_K * (pre_activation + GELU_C * pre_activation * pre_activation * pre_activation))
    value_out = 0.5 * pre_activation * (1.0 + tangent)
    slopes = 0.5 * (1.0 + tangent) + 0.5 * pre_activation * (1.0 - tangent * tangent) * GELU_K * (1.0 + 3.0 * GELU_C * pre_activation * pre_activation)
    return (value_out, slopes)

def reference(tokens, cotangent, frozen_in, frozen_out, input_adapter_first, input_adapter_second, adapter_out_a, adapter_out_b):
    highest_precision = lax.Precision.HIGHEST
    gradient_scale = ADAPTER_SCALE / math.sqrt(TOKEN_COUNT)
    lowrank_input = jnp.dot(tokens, input_adapter_first, preferred_element_type=jnp.float32)
    backward_lowrank = jnp.dot(cotangent, adapter_out_b.T, preferred_element_type=jnp.float32)
    block_width = FF // N_HID

    def one_block(running, block_index):
        rank_sum, back_sum, dense_total_sum = running
        begin_at = (block_index * block_width).astype(jnp.int32)
        input_weight = lax.dynamic_slice_in_dim(frozen_in, begin_at, block_width, 1)
        input_second_factor = lax.dynamic_slice_in_dim(input_adapter_second, begin_at, block_width, 1)
        output_adapter_first = lax.dynamic_slice_in_dim(adapter_out_a, begin_at, block_width, 0)
        output_weight = lax.dynamic_slice_in_dim(frozen_out, begin_at, block_width, 0)
        pre_activation = jnp.dot(tokens, input_weight, preferred_element_type=jnp.float32) + ADAPTER_SCALE * jnp.dot(lowrank_input, input_second_factor.astype(jnp.float32), precision=highest_precision)
        value_out, slopes = gelu_pair(pre_activation)
        hidden_act = value_out.astype(jnp.bfloat16)
        rank_sum = rank_sum + jnp.dot(hidden_act, output_adapter_first, preferred_element_type=jnp.float32)
        dense_backward = jnp.dot(cotangent, output_weight.T, preferred_element_type=jnp.float32) + ADAPTER_SCALE * jnp.dot(backward_lowrank, output_adapter_first.astype(jnp.float32).T, precision=highest_precision)
        grad_pre = (dense_backward * slopes).astype(jnp.bfloat16)
        back_sum = back_sum + jnp.dot(grad_pre, input_second_factor.T, preferred_element_type=jnp.float32)
        dense_total_sum = dense_total_sum + jnp.dot(grad_pre, input_weight.T, preferred_element_type=jnp.float32)
        grad_oa = gradient_scale * jnp.dot(hidden_act.astype(jnp.float32).T, backward_lowrank, precision=highest_precision)
        grad_ib = gradient_scale * jnp.dot(lowrank_input.T, grad_pre.astype(jnp.float32), precision=highest_precision)
        return ((rank_sum, back_sum, dense_total_sum), (grad_oa, grad_ib))
    initial = (jnp.zeros((TOKEN_COUNT, RANK), jnp.float32), jnp.zeros((TOKEN_COUNT, RANK), jnp.float32), jnp.zeros((TOKEN_COUNT, D), jnp.float32))
    (rank_out, rank_backward, dense_total_sum), (oa_blocks, ib_blocks) = lax.scan(one_block, initial, jnp.arange(N_HID, dtype=jnp.int32))
    grad_out_a = oa_blocks.reshape(FF, RANK)
    grad_in_b = jnp.transpose(ib_blocks, (1, 0, 2)).reshape(RANK, FF)
    input_gradient = dense_total_sum + ADAPTER_SCALE * jnp.dot(rank_backward, input_adapter_first.astype(jnp.float32).T, precision=highest_precision)
    grad_out_b = gradient_scale * jnp.dot(rank_out.T, cotangent.astype(jnp.float32), precision=highest_precision)
    grad_in_a = gradient_scale * jnp.dot(tokens.astype(jnp.float32).T, rank_backward, precision=highest_precision)
    return (input_gradient, grad_in_a, grad_in_b, grad_out_a, grad_out_b)
```

```python
import math

import jax
import jax.numpy as jnp
from jax import lax
from jax.sharding import PartitionSpec as P

ADAPTER_SCALE = 0.5
GELU_K = 0.7978845608
GELU_C = 0.044715
F32 = jnp.float32
BF16 = jnp.bfloat16


def gelu_pair(pre_activation):
    tangent = jnp.tanh(
        GELU_K * (pre_activation + GELU_C * pre_activation * pre_activation * pre_activation)
    )
    value_out = 0.5 * pre_activation * (1.0 + tangent)
    slopes = 0.5 * (1.0 + tangent) + 0.5 * pre_activation * (1.0 - tangent * tangent) * GELU_K * (
        1.0 + 3.0 * GELU_C * pre_activation * pre_activation
    )
    return (value_out, slopes)


def halves(value):
    high = lax.reduce_precision(value, exponent_bits=8, mantissa_bits=7)
    return jnp.concatenate([high.astype(BF16), (value - high).astype(BF16)], axis=1)


def dot(left, right, dims):
    return lax.dot_general(left, right, (dims, ((), ())), preferred_element_type=F32)


def gather_inputs(tokens, cotangent, frozen_in, frozen_out, in_a):
    rows, rank = tokens.shape[0], in_a.shape[1]
    n_tok = lax.axis_size("tok")
    both = lax.all_gather(jnp.stack([tokens, cotangent]), "tok", axis=1, tiled=True)
    both = lax.all_gather(both, "hid", axis=2, tiled=True)
    in_a_full = lax.all_gather(in_a, "hid", axis=0, tiled=True)
    w_in = lax.all_to_all(frozen_in, "tok", split_axis=1, concat_axis=0, tiled=True)
    w_out = lax.all_to_all(frozen_out, "tok", split_axis=0, concat_axis=1, tiled=True)
    return both[0], both[1], w_in, w_out, in_a_full


def reduce_outputs(dense, terms):
    n_tok, n_hid = lax.axis_size("tok"), lax.axis_size("hid")
    stacked = jnp.concatenate([dense, terms], axis=0).astype(BF16)
    split = lax.all_to_all(
        stacked.reshape(stacked.shape[0], n_hid, -1).transpose(1, 0, 2),
        "hid", split_axis=0, concat_axis=0, tiled=True,
    )
    over_hid = jnp.sum(split.astype(F32), axis=0).astype(BF16)
    count = dense.shape[0]
    mine = over_hid[:count].reshape(n_tok, count // n_tok, -1)
    shared = jnp.broadcast_to(over_hid[count:], (n_tok,) + over_hid[count:].shape)
    over_tok = lax.all_to_all(
        jnp.concatenate([mine, shared], axis=1), "tok", split_axis=0, concat_axis=0, tiled=True
    )
    total = jnp.sum(over_tok.astype(F32), axis=0)
    return total[: count // n_tok], total[count // n_tok :]


def local(tokens, cotangent, frozen_in, frozen_out, in_a, in_b, out_a, out_b):
    n_tok, t = lax.axis_size("tok"), lax.axis_index("tok")
    rank = in_b.shape[0]
    count = tokens.shape[0] * n_tok
    scale = ADAPTER_SCALE / math.sqrt(count)
    width = frozen_in.shape[1] // n_tok
    x, c, w_in, w_out, in_a_full = gather_inputs(tokens, cotangent, frozen_in, frozen_out, in_a)
    second = lax.dynamic_slice_in_dim(in_b, t * width, width, 1)
    first = lax.dynamic_slice_in_dim(out_a, t * width, width, 0)
    half_second = (ADAPTER_SCALE * second).astype(BF16)
    half_first = (ADAPTER_SCALE * first).astype(BF16)
    half_in_a = (ADAPTER_SCALE * in_a_full).astype(BF16)
    low_in = halves(dot(x, in_a_full, ((1,), (0,))))
    back_low = halves(dot(c, out_b, ((1,), (1,))))
    pre = dot(x, w_in, ((1,), (0,))) + dot(
        low_in, jnp.concatenate([half_second, half_second], axis=0), ((1,), (0,))
    )
    value_out, slopes = gelu_pair(pre)
    act = value_out.astype(BF16)
    dense_back = dot(c, w_out, ((1,), (1,))) + dot(
        back_low, jnp.concatenate([half_first, half_first], axis=1), ((1,), (1,))
    )
    grad_pre = (dense_back * slopes).astype(BF16)
    oa = dot(act, back_low, ((0,), (0,)))
    oa = scale * (oa[:, :rank] + oa[:, rank:])
    ib = dot(low_in, grad_pre, ((0,), (0,)))
    ib = scale * (ib[:rank] + ib[rank:])
    grad_out_a = lax.all_gather(oa.astype(BF16), "tok", axis=0, tiled=True).astype(F32)
    grad_in_b = lax.all_gather(ib.astype(BF16), "tok", axis=1, tiled=True).astype(F32)
    rank_out = halves(dot(act, first, ((1,), (0,))))
    rank_back = halves(dot(grad_pre, second, ((1,), (1,))))
    dense = dot(grad_pre, w_in, ((1,), (1,))) + dot(
        rank_back, jnp.concatenate([half_in_a, half_in_a], axis=1), ((1,), (1,))
    )
    out_term = dot(rank_out, c, ((0,), (0,)))
    in_term = dot(rank_back, x, ((0,), (0,)))
    terms = scale * jnp.concatenate(
        [out_term[:rank] + out_term[rank:], in_term[:rank] + in_term[rank:]], axis=0
    )
    input_gradient, total = reduce_outputs(dense, terms)
    return (input_gradient, total[rank:].T, grad_in_b, grad_out_a, total[:rank])


def local_by_rows(
    tokens,
    cotangent,
    frozen_in,
    frozen_out,
    input_adapter_first,
    input_adapter_second,
    adapter_out_a,
    adapter_out_b,
):
    highest_precision = lax.Precision.HIGHEST
    device_local_rows = tokens.shape[0]
    rank_width = input_adapter_second.shape[0]
    gradient_scale = ADAPTER_SCALE / math.sqrt(device_local_rows * lax.axis_size("tok"))
    full_tokens, full_cotan = (
        lax.all_gather(tokens, "hid", axis=1, tiled=True),
        lax.all_gather(cotangent, "hid", axis=1, tiled=True),
    )
    in_rows = lax.all_gather(frozen_in, "tok", axis=0, tiled=True)
    in_a_full = lax.all_gather(input_adapter_first, "hid", axis=0, tiled=True)
    lowrank_input = jnp.dot(full_tokens, in_a_full, preferred_element_type=jnp.float32)
    second_float = input_adapter_second.astype(jnp.float32)
    out_a_float = adapter_out_a.astype(jnp.float32)
    pre_activation = jnp.dot(
        full_tokens, in_rows, preferred_element_type=jnp.float32
    ) + ADAPTER_SCALE * jnp.dot(lowrank_input, second_float, precision=highest_precision)
    value_out, slopes = gelu_pair(pre_activation)
    hidden_act = value_out.astype(jnp.bfloat16)
    backward_lowrank = jnp.einsum(
        "td,rd->tr", full_cotan, adapter_out_b, preferred_element_type=jnp.float32
    )
    rank_out = jnp.dot(hidden_act, adapter_out_a, preferred_element_type=jnp.float32)
    dense_backward = jnp.einsum(
        "td,fd->tf",
        full_cotan,
        lax.all_gather(frozen_out, "tok", axis=1, tiled=True),
        preferred_element_type=jnp.float32,
    )
    dense_backward = dense_backward + ADAPTER_SCALE * jnp.dot(
        backward_lowrank, out_a_float.T, precision=highest_precision
    )
    grad_pre = (dense_backward * slopes).astype(jnp.bfloat16)
    rank_backward = jnp.einsum(
        "tf,rf->tr", grad_pre, input_adapter_second, preferred_element_type=jnp.float32
    )
    dense_in = jnp.einsum("tf,df->td", grad_pre, in_rows, preferred_element_type=jnp.float32)
    grad_out_a = gradient_scale * jnp.dot(
        hidden_act.astype(jnp.float32).T, backward_lowrank, precision=highest_precision
    )
    grad_in_b = gradient_scale * jnp.dot(
        lowrank_input.T, grad_pre.astype(jnp.float32), precision=highest_precision
    )
    in_a_float = in_a_full.astype(jnp.float32)
    dx_term = dense_in + ADAPTER_SCALE * jnp.dot(
        rank_backward, in_a_float.T, precision=highest_precision
    )
    out_term = jnp.dot(rank_out.T, full_cotan.astype(jnp.float32), precision=highest_precision)
    in_term = jnp.dot(rank_backward.T, full_tokens.astype(jnp.float32), precision=highest_precision)
    rank_terms = jnp.concatenate([out_term, in_term], axis=0)
    input_gradient, rank_local = (
        lax.psum_scatter(dx_term, "hid", scatter_dimension=1, tiled=True),
        lax.psum_scatter(rank_terms, "hid", scatter_dimension=1, tiled=True),
    )
    grad_out_a, grad_in_b, rank_total = lax.psum((grad_out_a, grad_in_b, rank_local), "tok")
    grad_out_b = gradient_scale * rank_total[:rank_width]
    grad_in_a = gradient_scale * rank_total[rank_width:].T
    return (input_gradient, grad_in_a, grad_in_b, grad_out_a, grad_out_b)


def solution(mesh):
    in_specs = (
        P("tok", "hid"),
        P("tok", "hid"),
        P("tok", "hid"),
        P("hid", "tok"),
        P("hid", None),
        P(None, "hid"),
        P("hid", None),
        P(),
    )
    out_specs = (P("tok", "hid"), P("hid", None), P(None, "hid"), P("hid", None), P(None, "hid"))
    def body(*arrays):
        share = arrays[2].shape[1] // lax.axis_size("tok")
        return local(*arrays) if share % 128 == 0 else local_by_rows(*arrays)

    return jax.shard_map(body, mesh=mesh, in_specs=in_specs, out_specs=out_specs, check_vma=False)
```

```python
import functools
import math

import jax
import jax.numpy as jnp
from jax import lax
from jax.experimental import pallas as pl
from jax.experimental.pallas import tpu as pltpu
from jax.sharding import PartitionSpec as P

ADAPTER_SCALE = 0.5
GELU_K = 0.7978845608
GELU_C = 0.044715
F32 = jnp.float32
BF16 = jnp.bfloat16


def gelu_pair(pre_activation):
    tangent = jnp.tanh(
        GELU_K * (pre_activation + GELU_C * pre_activation * pre_activation * pre_activation)
    )
    value_out = 0.5 * pre_activation * (1.0 + tangent)
    slopes = 0.5 * (1.0 + tangent) + 0.5 * pre_activation * (1.0 - tangent * tangent) * GELU_K * (
        1.0 + 3.0 * GELU_C * pre_activation * pre_activation
    )
    return (value_out, slopes)


def halves(value):
    high = lax.reduce_precision(value, exponent_bits=8, mantissa_bits=7)
    return jnp.concatenate([high.astype(BF16), (value - high).astype(BF16)], axis=1)


def dot(left, right, dims):
    return lax.dot_general(left, right, (dims, ((), ())), preferred_element_type=F32)


def gather_inputs(tokens, cotangent, frozen_in, frozen_out, in_a):
    rows, rank = tokens.shape[0], in_a.shape[1]
    n_tok = lax.axis_size("tok")
    both = lax.all_gather(jnp.stack([tokens, cotangent]), "tok", axis=1, tiled=True)
    both = lax.all_gather(both, "hid", axis=2, tiled=True)
    in_a_full = lax.all_gather(in_a, "hid", axis=0, tiled=True)
    w_in = lax.all_to_all(frozen_in, "tok", split_axis=1, concat_axis=0, tiled=True)
    w_out = lax.all_to_all(frozen_out, "tok", split_axis=0, concat_axis=1, tiled=True)
    return both[0], both[1], w_in, w_out, in_a_full


def reduce_kernel(
    n_tok, n_hid, dense, terms, oa, ib,
    dx_out, terms_out, oa_out, ib_out,
    core_d, core_t, send_d, send_t, recv_d, recv_t, kept_d, kept_t, tok_send, tok_recv,
    all_t, all_oa, all_ib,
    core_sem, chip_sem, tok_sem, term_sem, grad_sem,
):
    t, h = lax.axis_index("tok"), lax.axis_index("hid")
    n_chip = n_hid // 2
    chip, core = h // 2, h % 2
    rows, cols = dx_out.shape
    count = terms.shape[0]
    width = oa.shape[0]

    def remote(source, target, sems, where):
        return pltpu.make_async_remote_copy(
            src_ref=source, dst_ref=target, send_sem=sems[0], recv_sem=sems[1],
            device_id=where, device_id_type=pl.DeviceIdType.MESH,
        )

    sibling = (t, 2 * chip + 1 - core)
    chips = [(t, 2 * ((chip + e) % n_chip) + core) for e in range(n_chip)]
    toks = [((t + d) % n_tok, h) for d in range(n_tok)]
    barrier = pltpu.get_barrier_semaphore()
    for where in [sibling] + chips[1:] + toks[1:]:
        pl.semaphore_signal(barrier, inc=1, device_id=where, device_id_type=pl.DeviceIdType.MESH)
    pl.semaphore_wait(barrier, n_chip + n_tok - 1)

    def block(index, parity):
        return pl.ds(pl.multiple_of((2 * index + parity) * cols, cols), cols)

    def tok_rows(d):
        return pl.ds(pl.multiple_of(((t + d) % n_tok) * rows, rows), rows)

    chunks = [None] + list(range(1, n_tok)) + [0]
    core_copies, chip_copies, tok_copies = [], [], []
    for q, d in enumerate(chunks):
        group = []
        for e in range(n_chip):
            columns = block((chip + e) % n_chip, 1 - core)
            source = terms.at[:, columns] if d is None else dense.at[tok_rows(d), columns]
            target = core_t.at[e] if d is None else core_d.at[d, e]
            copy = remote(source, target, (core_sem.at[0, q, e], core_sem.at[1, q, e]), sibling)
            copy.start()
            group.append(copy)
        core_copies.append(group)
    for d in range(1, n_tok):
        for k, (source, target) in enumerate(((oa, all_oa), (ib, all_ib))):
            copy = remote(
                source, target.at[t], (grad_sem.at[0, d - 1, k], grad_sem.at[1, d - 1, k]), toks[d]
            )
            copy.start()
            tok_copies.append(copy)

    def over_core(q):
        d, group = chunks[q], []
        for e in range(n_chip):
            core_copies[q][e].wait_recv()
            columns = block((chip + e) % n_chip, core)
            if d is None:
                value = terms[:, columns] + core_t[e]
            else:
                value = dense[tok_rows(d), columns] + core_d[d, e]
            if e == 0:
                if d is None:
                    kept_t[...] = value
                else:
                    kept_d[d] = value
                continue
            sent, got = (send_t, recv_t) if d is None else (send_d.at[d], recv_d.at[d])
            sent[e - 1] = value.astype(BF16)
            copy = remote(
                sent.at[e - 1], got.at[e - 1],
                (chip_sem.at[0, q, e - 1], chip_sem.at[1, q, e - 1]), chips[e],
            )
            copy.start()
            group.append(copy)
        chip_copies.append(group)

    def over_chips(q):
        d = chunks[q]
        for copy in chip_copies[q]:
            copy.wait_recv()
        got = recv_t if d is None else recv_d.at[d]
        value = kept_t[...] if d is None else kept_d[d]
        for e in range(n_chip - 1):
            value = value + got[e].astype(F32)
        if d is None:
            all_t[t] = value.astype(BF16)
            for k in range(1, n_tok):
                copy = remote(
                    all_t.at[t], all_t.at[t], (term_sem.at[0, k - 1], term_sem.at[1, k - 1]), toks[k]
                )
                copy.start()
                tok_copies.append(copy)
        elif d == 0:
            kept_d[0] = value
        else:
            tok_send[d - 1] = value.astype(BF16)
            copy = remote(
                tok_send.at[d - 1], tok_recv.at[d - 1],
                (tok_sem.at[0, d - 1], tok_sem.at[1, d - 1]), toks[d],
            )
            copy.start()
            tok_copies.append(copy)

    over_core(0)
    for q in range(1, n_tok + 1):
        over_core(q)
        over_chips(q - 1)
    all_oa[t] = oa[...]
    all_ib[t] = ib[...]
    over_chips(n_tok)
    for copy in tok_copies:
        copy.wait_recv()
    for k in range(n_tok):
        oa_out[pl.ds(k * width, width), :] = all_oa[k].astype(F32)
        ib_out[:, pl.ds(k * width, width)] = all_ib[k].astype(F32)
    value = all_t[0].astype(F32)
    for k in range(1, n_tok):
        value = value + all_t[k].astype(F32)
    terms_out[...] = value
    value = kept_d[0]
    for d in range(1, n_tok):
        value = value + tok_recv[d - 1].astype(F32)
    dx_out[...] = value
    for group in core_copies + chip_copies + [tok_copies]:
        for copy in group:
            copy.wait_send()


def reduce_outputs(dense, terms, oa, ib):
    n_tok, n_hid = lax.axis_size("tok"), lax.axis_size("hid")
    n_chip = n_hid // 2
    rows, cols = dense.shape[0] // n_tok, dense.shape[1] // n_hid
    count = terms.shape[0]
    width, rank = oa.shape
    sems = pltpu.SemaphoreType.DMA
    vmem = pl.BlockSpec(memory_space=pltpu.VMEM)
    return pl.pallas_call(
        functools.partial(reduce_kernel, n_tok, n_hid),
        out_shape=(
            jax.ShapeDtypeStruct((rows, cols), F32),
            jax.ShapeDtypeStruct((count, cols), F32),
            jax.ShapeDtypeStruct((n_tok * width, rank), F32),
            jax.ShapeDtypeStruct((rank, n_tok * width), F32),
        ),
        in_specs=[vmem] * 4,
        out_specs=(vmem,) * 4,
        scratch_shapes=[
            pltpu.VMEM((n_tok, n_chip, rows, cols), F32),
            pltpu.VMEM((n_chip, count, cols), F32),
            pltpu.VMEM((n_tok, n_chip - 1, rows, cols), BF16),
            pltpu.VMEM((n_chip - 1, count, cols), BF16),
            pltpu.VMEM((n_tok, n_chip - 1, rows, cols), BF16),
            pltpu.VMEM((n_chip - 1, count, cols), BF16),
            pltpu.VMEM((n_tok, rows, cols), F32),
            pltpu.VMEM((count, cols), F32),
            pltpu.VMEM((n_tok - 1, rows, cols), BF16),
            pltpu.VMEM((n_tok - 1, rows, cols), BF16),
            pltpu.VMEM((n_tok, count, cols), BF16),
            pltpu.VMEM((n_tok, width, rank), BF16),
            pltpu.VMEM((n_tok, rank, width), BF16),
            sems((2, n_tok + 1, n_chip)),
            sems((2, n_tok + 1, n_chip - 1)),
            sems((2, n_tok - 1)),
            sems((2, n_tok - 1)),
            sems((2, n_tok - 1, 2)),
        ],
        compiler_params=pltpu.CompilerParams(
            collective_id=1, has_side_effects=True, vmem_limit_bytes=56 * 1024 * 1024
        ),
    )(dense, terms, oa, ib)


def local(tokens, cotangent, frozen_in, frozen_out, in_a, in_b, out_a, out_b):
    n_tok, t = lax.axis_size("tok"), lax.axis_index("tok")
    rank = in_b.shape[0]
    count = tokens.shape[0] * n_tok
    scale = ADAPTER_SCALE / math.sqrt(count)
    width = frozen_in.shape[1] // n_tok
    x, c, w_in, w_out, in_a_full = gather_inputs(tokens, cotangent, frozen_in, frozen_out, in_a)
    second = lax.dynamic_slice_in_dim(in_b, t * width, width, 1)
    first = lax.dynamic_slice_in_dim(out_a, t * width, width, 0)
    half_second = (ADAPTER_SCALE * second).astype(BF16)
    half_first = (ADAPTER_SCALE * first).astype(BF16)
    half_in_a = (ADAPTER_SCALE * in_a_full).astype(BF16)
    low_in = halves(dot(x, in_a_full, ((1,), (0,))))
    back_low = halves(dot(c, out_b, ((1,), (1,))))
    pre = dot(x, w_in, ((1,), (0,))) + dot(
        low_in, jnp.concatenate([half_second, half_second], axis=0), ((1,), (0,))
    )
    value_out, slopes = gelu_pair(pre)
    act = value_out.astype(BF16)
    dense_back = dot(c, w_out, ((1,), (1,))) + dot(
        back_low, jnp.concatenate([half_first, half_first], axis=1), ((1,), (1,))
    )
    grad_pre = (dense_back * slopes).astype(BF16)
    oa = dot(act, back_low, ((0,), (0,)))
    oa = scale * (oa[:, :rank] + oa[:, rank:])
    ib = dot(low_in, grad_pre, ((0,), (0,)))
    ib = scale * (ib[:rank] + ib[rank:])
    rank_out = halves(dot(act, first, ((1,), (0,))))
    rank_back = halves(dot(grad_pre, second, ((1,), (1,))))
    dense = dot(grad_pre, w_in, ((1,), (1,))) + dot(
        rank_back, jnp.concatenate([half_in_a, half_in_a], axis=1), ((1,), (1,))
    )
    out_term = dot(rank_out, c, ((0,), (0,)))
    in_term = dot(rank_back, x, ((0,), (0,)))
    terms = scale * jnp.concatenate(
        [out_term[:rank] + out_term[rank:], in_term[:rank] + in_term[rank:]], axis=0
    )
    input_gradient, total, grad_out_a, grad_in_b = reduce_outputs(
        dense, terms, oa.astype(BF16), ib.astype(BF16)
    )
    return (input_gradient, total[rank:].T, grad_in_b, grad_out_a, total[:rank])


def local_by_rows(
    tokens,
    cotangent,
    frozen_in,
    frozen_out,
    input_adapter_first,
    input_adapter_second,
    adapter_out_a,
    adapter_out_b,
):
    highest_precision = lax.Precision.HIGHEST
    device_local_rows = tokens.shape[0]
    rank_width = input_adapter_second.shape[0]
    gradient_scale = ADAPTER_SCALE / math.sqrt(device_local_rows * lax.axis_size("tok"))
    full_tokens, full_cotan = (
        lax.all_gather(tokens, "hid", axis=1, tiled=True),
        lax.all_gather(cotangent, "hid", axis=1, tiled=True),
    )
    in_rows = lax.all_gather(frozen_in, "tok", axis=0, tiled=True)
    in_a_full = lax.all_gather(input_adapter_first, "hid", axis=0, tiled=True)
    lowrank_input = jnp.dot(full_tokens, in_a_full, preferred_element_type=jnp.float32)
    second_float = input_adapter_second.astype(jnp.float32)
    out_a_float = adapter_out_a.astype(jnp.float32)
    pre_activation = jnp.dot(
        full_tokens, in_rows, preferred_element_type=jnp.float32
    ) + ADAPTER_SCALE * jnp.dot(lowrank_input, second_float, precision=highest_precision)
    value_out, slopes = gelu_pair(pre_activation)
    hidden_act = value_out.astype(jnp.bfloat16)
    backward_lowrank = jnp.einsum(
        "td,rd->tr", full_cotan, adapter_out_b, preferred_element_type=jnp.float32
    )
    rank_out = jnp.dot(hidden_act, adapter_out_a, preferred_element_type=jnp.float32)
    dense_backward = jnp.einsum(
        "td,fd->tf",
        full_cotan,
        lax.all_gather(frozen_out, "tok", axis=1, tiled=True),
        preferred_element_type=jnp.float32,
    )
    dense_backward = dense_backward + ADAPTER_SCALE * jnp.dot(
        backward_lowrank, out_a_float.T, precision=highest_precision
    )
    grad_pre = (dense_backward * slopes).astype(jnp.bfloat16)
    rank_backward = jnp.einsum(
        "tf,rf->tr", grad_pre, input_adapter_second, preferred_element_type=jnp.float32
    )
    dense_in = jnp.einsum("tf,df->td", grad_pre, in_rows, preferred_element_type=jnp.float32)
    grad_out_a = gradient_scale * jnp.dot(
        hidden_act.astype(jnp.float32).T, backward_lowrank, precision=highest_precision
    )
    grad_in_b = gradient_scale * jnp.dot(
        lowrank_input.T, grad_pre.astype(jnp.float32), precision=highest_precision
    )
    in_a_float = in_a_full.astype(jnp.float32)
    dx_term = dense_in + ADAPTER_SCALE * jnp.dot(
        rank_backward, in_a_float.T, precision=highest_precision
    )
    out_term = jnp.dot(rank_out.T, full_cotan.astype(jnp.float32), precision=highest_precision)
    in_term = jnp.dot(rank_backward.T, full_tokens.astype(jnp.float32), precision=highest_precision)
    rank_terms = jnp.concatenate([out_term, in_term], axis=0)
    input_gradient, rank_local = (
        lax.psum_scatter(dx_term, "hid", scatter_dimension=1, tiled=True),
        lax.psum_scatter(rank_terms, "hid", scatter_dimension=1, tiled=True),
    )
    grad_out_a, grad_in_b, rank_total = lax.psum((grad_out_a, grad_in_b, rank_local), "tok")
    grad_out_b = gradient_scale * rank_total[:rank_width]
    grad_in_a = gradient_scale * rank_total[rank_width:].T
    return (input_gradient, grad_in_a, grad_in_b, grad_out_a, grad_out_b)


def solution(mesh):
    in_specs = (
        P("tok", "hid"),
        P("tok", "hid"),
        P("tok", "hid"),
        P("hid", "tok"),
        P("hid", None),
        P(None, "hid"),
        P("hid", None),
        P(),
    )
    out_specs = (P("tok", "hid"), P("hid", None), P(None, "hid"), P("hid", None), P(None, "hid"))
    def body(*arrays):
        share = arrays[2].shape[1] // lax.axis_size("tok")
        return local(*arrays) if share % 128 == 0 else local_by_rows(*arrays)

    return jax.shard_map(body, mesh=mesh, in_specs=in_specs, out_specs=out_specs, check_vma=False)
```

```python
import functools
import math

import jax
import jax.numpy as jnp
from jax import lax
from jax.experimental import pallas as pl
from jax.experimental.pallas import tpu as pltpu
from jax.sharding import PartitionSpec as P

ADAPTER_SCALE = 0.5
GELU_K = 0.7978845608
GELU_C = 0.044715
F32 = jnp.float32
BF16 = jnp.bfloat16


def gelu_pair(pre_activation):
    tangent = jnp.tanh(
        GELU_K * (pre_activation + GELU_C * pre_activation * pre_activation * pre_activation)
    )
    value_out = 0.5 * pre_activation * (1.0 + tangent)
    slopes = 0.5 * (1.0 + tangent) + 0.5 * pre_activation * (1.0 - tangent * tangent) * GELU_K * (
        1.0 + 3.0 * GELU_C * pre_activation * pre_activation
    )
    return (value_out, slopes)


def halves(value):
    high = lax.reduce_precision(value, exponent_bits=8, mantissa_bits=7)
    return jnp.concatenate([high.astype(BF16), (value - high).astype(BF16)], axis=1)


def dot(left, right, dims):
    return lax.dot_general(left, right, (dims, ((), ())), preferred_element_type=F32)


def gather_kernel(
    n_tok, n_hid, tokens, cotangent, w_in, w_out, in_a,
    x, c, full_in, full_out, full_a,
    tok_sem, chip_sem, core_sem, first_sem, first_core_sem, own_sem,
):
    t, h = lax.axis_index("tok"), lax.axis_index("hid")
    n_chip = n_hid // 2
    chip, core = h // 2, h % 2
    rows, cols = tokens.shape
    depth = w_in.shape[0]
    width = full_in.shape[1]

    def remote(source, target, sems, where):
        copy = pltpu.make_async_remote_copy(
            src_ref=source, dst_ref=target, send_sem=sems[0], recv_sem=sems[1],
            device_id=where, device_id_type=pl.DeviceIdType.MESH,
        )
        copy.start()
        return copy

    def pair(sems, *where):
        return sems.at[(0,) + where], sems.at[(1,) + where]

    sibling = (t, 2 * chip + 1 - core)
    chips = [(t, 2 * ((chip + e) % n_chip) + core) for e in range(n_chip)]
    toks = [((t + d) % n_tok, h) for d in range(n_tok)]
    barrier = pltpu.get_barrier_semaphore()
    for where in [sibling] + chips[1:] + toks[1:]:
        pl.semaphore_signal(barrier, inc=1, device_id=where, device_id_type=pl.DeviceIdType.MESH)
    pl.semaphore_wait(barrier, n_chip + n_tok - 1)

    def part(array, d, e):
        at_row = pl.multiple_of(((t + n_tok - d) % n_tok) * rows, rows)
        at_col = pl.multiple_of((2 * ((chip + n_chip - e) % n_chip) + core) * cols, cols)
        return array.at[pl.ds(at_row, rows), pl.ds(at_col, cols)]

    def first_part(e):
        at = pl.multiple_of((2 * ((chip + n_chip - e) % n_chip) + core) * cols, cols)
        return full_a.at[pl.ds(at, cols), :]

    both = ((tokens, x), (cotangent, c))
    sent, from_tok, from_chip, from_core, weights = [], [], [], [], []
    for d in range(1, n_tok):
        from_tok.append([
            remote(own, part(whole, 0, 0), pair(tok_sem, d - 1, k), toks[d])
            for k, (own, whole) in enumerate(both)
        ])

    def to_chips(d, blocks):
        from_chip.append([
            [
                remote(blocks[k], part(both[k][1], d, 0), pair(chip_sem, d, e - 1, k), chips[e])
                for k in range(2)
            ]
            for e in range(1, n_chip)
        ])

    def to_core(d, e, blocks):
        for k in range(2):
            from_core.append(
                remote(blocks[k], part(both[k][1], d, e), pair(core_sem, d, e, k), sibling)
            )

    to_chips(0, (tokens, cotangent))
    firsts = [
        remote(in_a, first_part(0), pair(first_sem, e - 1), chips[e]) for e in range(1, n_chip)
    ]
    to_core(0, 0, (tokens, cotangent))
    from_core.append(remote(in_a, first_part(0), pair(first_core_sem, 0), sibling))
    for d in range(1, n_tok):
        at = pl.multiple_of(((t + d) % n_tok) * width, width)
        depths = pl.ds(pl.multiple_of(t * depth, depth), depth)
        weights.append(remote(
            w_in.at[:, pl.ds(at, width)], full_in.at[depths, :], pair(tok_sem, d - 1, 2), toks[d]
        ))
        weights.append(remote(
            w_out.at[pl.ds(at, width), :], full_out.at[:, depths], pair(tok_sem, d - 1, 3), toks[d]
        ))
    at = pl.multiple_of(t * width, width)
    depths = pl.ds(pl.multiple_of(t * depth, depth), depth)
    own = [
        (tokens, part(x, 0, 0)),
        (cotangent, part(c, 0, 0)),
        (w_in.at[:, pl.ds(at, width)], full_in.at[depths, :]),
        (w_out.at[pl.ds(at, width), :], full_out.at[:, depths]),
        (in_a, first_part(0)),
    ]
    own = [
        pltpu.make_async_copy(source, target, own_sem.at[k])
        for k, (source, target) in enumerate(own)
    ]
    for copy in own:
        copy.start()

    def pass_on(d):
        for e in range(1, n_chip):
            for copy in from_chip[d][e - 1]:
                copy.wait_recv()
            to_core(d, e, (part(x, d, e), part(c, d, e)))

    for d in range(1, n_tok):
        for copy in from_tok[d - 1]:
            copy.wait_recv()
        blocks = (part(x, d, 0), part(c, d, 0))
        to_chips(d, blocks)
        to_core(d, 0, blocks)
        pass_on(d - 1)
    for e in range(1, n_chip):
        firsts[e - 1].wait_recv()
        from_core.append(remote(first_part(e), first_part(e), pair(first_core_sem, e), sibling))
    pass_on(n_tok - 1)
    for copy in from_core + weights:
        copy.wait_recv()
    for copy in own:
        copy.wait()
    for group in from_tok + [firsts, from_core, weights]:
        for copy in group:
            copy.wait_send()
    for groups in from_chip:
        for group in groups:
            for copy in group:
                copy.wait_send()


def gather_inputs(tokens, cotangent, frozen_in, frozen_out, in_a):
    n_tok, n_hid = lax.axis_size("tok"), lax.axis_size("hid")
    n_chip = n_hid // 2
    count, features = tokens.shape[0] * n_tok, tokens.shape[1] * n_hid
    width = frozen_in.shape[1] // n_tok
    sems = pltpu.SemaphoreType.DMA
    vmem = pl.BlockSpec(memory_space=pltpu.VMEM)
    whole = pl.BlockSpec(memory_space=pl.ANY)
    return pl.pallas_call(
        functools.partial(gather_kernel, n_tok, n_hid),
        out_shape=(
            jax.ShapeDtypeStruct((count, features), BF16),
            jax.ShapeDtypeStruct((count, features), BF16),
            jax.ShapeDtypeStruct((features, width), BF16),
            jax.ShapeDtypeStruct((width, features), BF16),
            jax.ShapeDtypeStruct((features, in_a.shape[1]), BF16),
        ),
        in_specs=[vmem] * 5,
        out_specs=(whole,) * 5,
        scratch_shapes=[
            sems((2, n_tok - 1, 4)),
            sems((2, n_tok, n_chip - 1, 2)),
            sems((2, n_tok, n_chip, 2)),
            sems((2, n_chip - 1)),
            sems((2, n_chip)),
            sems((5,)),
        ],
        compiler_params=pltpu.CompilerParams(
            collective_id=2, has_side_effects=True, vmem_limit_bytes=56 * 1024 * 1024
        ),
    )(tokens, cotangent, frozen_in, frozen_out, in_a)


def reduce_kernel(
    n_tok, n_hid, dense, terms, oa, ib,
    dx_out, terms_out, oa_out, ib_out,
    core_d, core_t, send_d, send_t, recv_d, recv_t, kept_d, kept_t, tok_send, tok_recv,
    all_t, all_oa, all_ib,
    core_sem, chip_sem, tok_sem, term_sem, grad_sem,
):
    t, h = lax.axis_index("tok"), lax.axis_index("hid")
    n_chip = n_hid // 2
    chip, core = h // 2, h % 2
    rows, cols = dx_out.shape
    count = terms.shape[0]
    width = oa.shape[0]

    def remote(source, target, sems, where):
        return pltpu.make_async_remote_copy(
            src_ref=source, dst_ref=target, send_sem=sems[0], recv_sem=sems[1],
            device_id=where, device_id_type=pl.DeviceIdType.MESH,
        )

    sibling = (t, 2 * chip + 1 - core)
    chips = [(t, 2 * ((chip + e) % n_chip) + core) for e in range(n_chip)]
    toks = [((t + d) % n_tok, h) for d in range(n_tok)]
    barrier = pltpu.get_barrier_semaphore()
    for where in [sibling] + chips[1:] + toks[1:]:
        pl.semaphore_signal(barrier, inc=1, device_id=where, device_id_type=pl.DeviceIdType.MESH)
    pl.semaphore_wait(barrier, n_chip + n_tok - 1)

    def block(index, parity):
        return pl.ds(pl.multiple_of((2 * index + parity) * cols, cols), cols)

    def tok_rows(d):
        return pl.ds(pl.multiple_of(((t + d) % n_tok) * rows, rows), rows)

    chunks = [None] + list(range(1, n_tok)) + [0]
    core_copies, chip_copies, tok_copies = [], [], []
    for q, d in enumerate(chunks):
        group = []
        for e in range(n_chip):
            columns = block((chip + e) % n_chip, 1 - core)
            source = terms.at[:, columns] if d is None else dense.at[tok_rows(d), columns]
            target = core_t.at[e] if d is None else core_d.at[d, e]
            copy = remote(source, target, (core_sem.at[0, q, e], core_sem.at[1, q, e]), sibling)
            copy.start()
            group.append(copy)
        core_copies.append(group)
    for d in range(1, n_tok):
        for k, (source, target) in enumerate(((oa, all_oa), (ib, all_ib))):
            copy = remote(
                source, target.at[t], (grad_sem.at[0, d - 1, k], grad_sem.at[1, d - 1, k]), toks[d]
            )
            copy.start()
            tok_copies.append(copy)

    def over_core(q):
        d, group = chunks[q], []
        for e in range(n_chip):
            core_copies[q][e].wait_recv()
            columns = block((chip + e) % n_chip, core)
            if d is None:
                value = terms[:, columns] + core_t[e]
            else:
                value = dense[tok_rows(d), columns] + core_d[d, e]
            if e == 0:
                if d is None:
                    kept_t[...] = value
                else:
                    kept_d[d] = value
                continue
            sent, got = (send_t, recv_t) if d is None else (send_d.at[d], recv_d.at[d])
            sent[e - 1] = value.astype(BF16)
            copy = remote(
                sent.at[e - 1], got.at[e - 1],
                (chip_sem.at[0, q, e - 1], chip_sem.at[1, q, e - 1]), chips[e],
            )
            copy.start()
            group.append(copy)
        chip_copies.append(group)

    def over_chips(q):
        d = chunks[q]
        for copy in chip_copies[q]:
            copy.wait_recv()
        got = recv_t if d is None else recv_d.at[d]
        value = kept_t[...] if d is None else kept_d[d]
        for e in range(n_chip - 1):
            value = value + got[e].astype(F32)
        if d is None:
            all_t[t] = value.astype(BF16)
            for k in range(1, n_tok):
                copy = remote(
                    all_t.at[t], all_t.at[t], (term_sem.at[0, k - 1], term_sem.at[1, k - 1]), toks[k]
                )
                copy.start()
                tok_copies.append(copy)
        elif d == 0:
            kept_d[0] = value
        else:
            tok_send[d - 1] = value.astype(BF16)
            copy = remote(
                tok_send.at[d - 1], tok_recv.at[d - 1],
                (tok_sem.at[0, d - 1], tok_sem.at[1, d - 1]), toks[d],
            )
            copy.start()
            tok_copies.append(copy)

    over_core(0)
    for q in range(1, n_tok + 1):
        over_core(q)
        over_chips(q - 1)
    all_oa[t] = oa[...]
    all_ib[t] = ib[...]
    over_chips(n_tok)
    for copy in tok_copies:
        copy.wait_recv()
    for k in range(n_tok):
        oa_out[pl.ds(k * width, width), :] = all_oa[k].astype(F32)
        ib_out[:, pl.ds(k * width, width)] = all_ib[k].astype(F32)
    value = all_t[0].astype(F32)
    for k in range(1, n_tok):
        value = value + all_t[k].astype(F32)
    terms_out[...] = value
    value = kept_d[0]
    for d in range(1, n_tok):
        value = value + tok_recv[d - 1].astype(F32)
    dx_out[...] = value
    for group in core_copies + chip_copies + [tok_copies]:
        for copy in group:
            copy.wait_send()


def reduce_outputs(dense, terms, oa, ib):
    n_tok, n_hid = lax.axis_size("tok"), lax.axis_size("hid")
    n_chip = n_hid // 2
    rows, cols = dense.shape[0] // n_tok, dense.shape[1] // n_hid
    count = terms.shape[0]
    width, rank = oa.shape
    sems = pltpu.SemaphoreType.DMA
    vmem = pl.BlockSpec(memory_space=pltpu.VMEM)
    return pl.pallas_call(
        functools.partial(reduce_kernel, n_tok, n_hid),
        out_shape=(
            jax.ShapeDtypeStruct((rows, cols), F32),
            jax.ShapeDtypeStruct((count, cols), F32),
            jax.ShapeDtypeStruct((n_tok * width, rank), F32),
            jax.ShapeDtypeStruct((rank, n_tok * width), F32),
        ),
        in_specs=[vmem] * 4,
        out_specs=(vmem,) * 4,
        scratch_shapes=[
            pltpu.VMEM((n_tok, n_chip, rows, cols), F32),
            pltpu.VMEM((n_chip, count, cols), F32),
            pltpu.VMEM((n_tok, n_chip - 1, rows, cols), BF16),
            pltpu.VMEM((n_chip - 1, count, cols), BF16),
            pltpu.VMEM((n_tok, n_chip - 1, rows, cols), BF16),
            pltpu.VMEM((n_chip - 1, count, cols), BF16),
            pltpu.VMEM((n_tok, rows, cols), F32),
            pltpu.VMEM((count, cols), F32),
            pltpu.VMEM((n_tok - 1, rows, cols), BF16),
            pltpu.VMEM((n_tok - 1, rows, cols), BF16),
            pltpu.VMEM((n_tok, count, cols), BF16),
            pltpu.VMEM((n_tok, width, rank), BF16),
            pltpu.VMEM((n_tok, rank, width), BF16),
            sems((2, n_tok + 1, n_chip)),
            sems((2, n_tok + 1, n_chip - 1)),
            sems((2, n_tok - 1)),
            sems((2, n_tok - 1)),
            sems((2, n_tok - 1, 2)),
        ],
        compiler_params=pltpu.CompilerParams(
            collective_id=1, has_side_effects=True, vmem_limit_bytes=56 * 1024 * 1024
        ),
    )(dense, terms, oa, ib)


def local(tokens, cotangent, frozen_in, frozen_out, in_a, in_b, out_a, out_b):
    n_tok, t = lax.axis_size("tok"), lax.axis_index("tok")
    rank = in_b.shape[0]
    count = tokens.shape[0] * n_tok
    scale = ADAPTER_SCALE / math.sqrt(count)
    width = frozen_in.shape[1] // n_tok
    x, c, w_in, w_out, in_a_full = gather_inputs(tokens, cotangent, frozen_in, frozen_out, in_a)
    second = lax.dynamic_slice_in_dim(in_b, t * width, width, 1)
    first = lax.dynamic_slice_in_dim(out_a, t * width, width, 0)
    half_second = (ADAPTER_SCALE * second).astype(BF16)
    half_first = (ADAPTER_SCALE * first).astype(BF16)
    half_in_a = (ADAPTER_SCALE * in_a_full).astype(BF16)
    low_in = halves(dot(x, in_a_full, ((1,), (0,))))
    back_low = halves(dot(c, out_b, ((1,), (1,))))
    pre = dot(x, w_in, ((1,), (0,))) + dot(
        low_in, jnp.concatenate([half_second, half_second], axis=0), ((1,), (0,))
    )
    value_out, slopes = gelu_pair(pre)
    act = value_out.astype(BF16)
    dense_back = dot(c, w_out, ((1,), (1,))) + dot(
        back_low, jnp.concatenate([half_first, half_first], axis=1), ((1,), (1,))
    )
    grad_pre = (dense_back * slopes).astype(BF16)
    oa = dot(act, back_low, ((0,), (0,)))
    oa = scale * (oa[:, :rank] + oa[:, rank:])
    ib = dot(low_in, grad_pre, ((0,), (0,)))
    ib = scale * (ib[:rank] + ib[rank:])
    rank_out = halves(dot(act, first, ((1,), (0,))))
    rank_back = halves(dot(grad_pre, second, ((1,), (1,))))
    dense = dot(grad_pre, w_in, ((1,), (1,))) + dot(
        rank_back, jnp.concatenate([half_in_a, half_in_a], axis=1), ((1,), (1,))
    )
    out_term = dot(rank_out, c, ((0,), (0,)))
    in_term = dot(rank_back, x, ((0,), (0,)))
    terms = scale * jnp.concatenate(
        [out_term[:rank] + out_term[rank:], in_term[:rank] + in_term[rank:]], axis=0
    )
    input_gradient, total, grad_out_a, grad_in_b = reduce_outputs(
        dense, terms, oa.astype(BF16), ib.astype(BF16)
    )
    return (input_gradient, total[rank:].T, grad_in_b, grad_out_a, total[:rank])


def local_by_rows(
    tokens,
    cotangent,
    frozen_in,
    frozen_out,
    input_adapter_first,
    input_adapter_second,
    adapter_out_a,
    adapter_out_b,
):
    highest_precision = lax.Precision.HIGHEST
    device_local_rows = tokens.shape[0]
    rank_width = input_adapter_second.shape[0]
    gradient_scale = ADAPTER_SCALE / math.sqrt(device_local_rows * lax.axis_size("tok"))
    full_tokens, full_cotan = (
        lax.all_gather(tokens, "hid", axis=1, tiled=True),
        lax.all_gather(cotangent, "hid", axis=1, tiled=True),
    )
    in_rows = lax.all_gather(frozen_in, "tok", axis=0, tiled=True)
    in_a_full = lax.all_gather(input_adapter_first, "hid", axis=0, tiled=True)
    lowrank_input = jnp.dot(full_tokens, in_a_full, preferred_element_type=jnp.float32)
    second_float = input_adapter_second.astype(jnp.float32)
    out_a_float = adapter_out_a.astype(jnp.float32)
    pre_activation = jnp.dot(
        full_tokens, in_rows, preferred_element_type=jnp.float32
    ) + ADAPTER_SCALE * jnp.dot(lowrank_input, second_float, precision=highest_precision)
    value_out, slopes = gelu_pair(pre_activation)
    hidden_act = value_out.astype(jnp.bfloat16)
    backward_lowrank = jnp.einsum(
        "td,rd->tr", full_cotan, adapter_out_b, preferred_element_type=jnp.float32
    )
    rank_out = jnp.dot(hidden_act, adapter_out_a, preferred_element_type=jnp.float32)
    dense_backward = jnp.einsum(
        "td,fd->tf",
        full_cotan,
        lax.all_gather(frozen_out, "tok", axis=1, tiled=True),
        preferred_element_type=jnp.float32,
    )
    dense_backward = dense_backward + ADAPTER_SCALE * jnp.dot(
        backward_lowrank, out_a_float.T, precision=highest_precision
    )
    grad_pre = (dense_backward * slopes).astype(jnp.bfloat16)
    rank_backward = jnp.einsum(
        "tf,rf->tr", grad_pre, input_adapter_second, preferred_element_type=jnp.float32
    )
    dense_in = jnp.einsum("tf,df->td", grad_pre, in_rows, preferred_element_type=jnp.float32)
    grad_out_a = gradient_scale * jnp.dot(
        hidden_act.astype(jnp.float32).T, backward_lowrank, precision=highest_precision
    )
    grad_in_b = gradient_scale * jnp.dot(
        lowrank_input.T, grad_pre.astype(jnp.float32), precision=highest_precision
    )
    in_a_float = in_a_full.astype(jnp.float32)
    dx_term = dense_in + ADAPTER_SCALE * jnp.dot(
        rank_backward, in_a_float.T, precision=highest_precision
    )
    out_term = jnp.dot(rank_out.T, full_cotan.astype(jnp.float32), precision=highest_precision)
    in_term = jnp.dot(rank_backward.T, full_tokens.astype(jnp.float32), precision=highest_precision)
    rank_terms = jnp.concatenate([out_term, in_term], axis=0)
    input_gradient, rank_local = (
        lax.psum_scatter(dx_term, "hid", scatter_dimension=1, tiled=True),
        lax.psum_scatter(rank_terms, "hid", scatter_dimension=1, tiled=True),
    )
    grad_out_a, grad_in_b, rank_total = lax.psum((grad_out_a, grad_in_b, rank_local), "tok")
    grad_out_b = gradient_scale * rank_total[:rank_width]
    grad_in_a = gradient_scale * rank_total[rank_width:].T
    return (input_gradient, grad_in_a, grad_in_b, grad_out_a, grad_out_b)


def solution(mesh):
    in_specs = (
        P("tok", "hid"),
        P("tok", "hid"),
        P("tok", "hid"),
        P("hid", "tok"),
        P("hid", None),
        P(None, "hid"),
        P("hid", None),
        P(),
    )
    out_specs = (P("tok", "hid"), P("hid", None), P(None, "hid"), P("hid", None), P(None, "hid"))
    def body(*arrays):
        share = arrays[2].shape[1] // lax.axis_size("tok")
        return local(*arrays) if share % 128 == 0 else local_by_rows(*arrays)

    return jax.shard_map(body, mesh=mesh, in_specs=in_specs, out_specs=out_specs, check_vma=False)
```

```python
import functools
import math

import jax
import jax.numpy as jnp
from jax import lax
from jax.experimental import pallas as pl
from jax.experimental.pallas import tpu as pltpu
from jax.sharding import PartitionSpec as P

ADAPTER_SCALE = 0.5
GELU_K = 0.7978845608
GELU_C = 0.044715
F32 = jnp.float32
BF16 = jnp.bfloat16


def gelu_pair(pre_activation):
    tangent = jnp.tanh(
        GELU_K * (pre_activation + GELU_C * pre_activation * pre_activation * pre_activation)
    )
    value_out = 0.5 * pre_activation * (1.0 + tangent)
    slopes = 0.5 * (1.0 + tangent) + 0.5 * pre_activation * (1.0 - tangent * tangent) * GELU_K * (
        1.0 + 3.0 * GELU_C * pre_activation * pre_activation
    )
    return (value_out, slopes)


def halves(value):
    high = lax.reduce_precision(value, exponent_bits=8, mantissa_bits=7)
    return jnp.concatenate([high.astype(BF16), (value - high).astype(BF16)], axis=1)


def dot(left, right, dims):
    return lax.dot_general(left, right, (dims, ((), ())), preferred_element_type=F32)


def gather_kernel(
    n_tok, n_hid, tokens, cotangent, w_in, w_out, in_a,
    x, c, full_in, full_out, full_a,
    tok_sem, chip_sem, core_sem, first_sem, first_core_sem, own_sem,
):
    t, h = lax.axis_index("tok"), lax.axis_index("hid")
    n_chip = n_hid // 2
    chip, core = h // 2, h % 2
    rows, cols = tokens.shape
    depth = w_in.shape[0]
    width = full_in.shape[1]

    def remote(source, target, sems, where):
        copy = pltpu.make_async_remote_copy(
            src_ref=source, dst_ref=target, send_sem=sems[0], recv_sem=sems[1],
            device_id=where, device_id_type=pl.DeviceIdType.MESH,
        )
        copy.start()
        return copy

    def pair(sems, *where):
        return sems.at[(0,) + where], sems.at[(1,) + where]

    sibling = (t, 2 * chip + 1 - core)
    chips = [(t, 2 * ((chip + e) % n_chip) + core) for e in range(n_chip)]
    toks = [((t + d) % n_tok, h) for d in range(n_tok)]
    barrier = pltpu.get_barrier_semaphore()
    for where in [sibling] + chips[1:] + toks[1:]:
        pl.semaphore_signal(barrier, inc=1, device_id=where, device_id_type=pl.DeviceIdType.MESH)
    pl.semaphore_wait(barrier, n_chip + n_tok - 1)

    def part(array, d, e):
        at_row = pl.multiple_of(((t + n_tok - d) % n_tok) * rows, rows)
        at_col = pl.multiple_of((2 * ((chip + n_chip - e) % n_chip) + core) * cols, cols)
        return array.at[pl.ds(at_row, rows), pl.ds(at_col, cols)]

    def first_part(e):
        at = pl.multiple_of((2 * ((chip + n_chip - e) % n_chip) + core) * cols, cols)
        return full_a.at[pl.ds(at, cols), :]

    both = ((tokens, x), (cotangent, c))
    sent, from_tok, from_chip, from_core, weights = [], [], [], [], []
    for d in range(1, n_tok):
        from_tok.append([
            remote(own, part(whole, 0, 0), pair(tok_sem, d - 1, k), toks[d])
            for k, (own, whole) in enumerate(both)
        ])

    def to_chips(d, blocks):
        from_chip.append([
            [
                remote(blocks[k], part(both[k][1], d, 0), pair(chip_sem, d, e - 1, k), chips[e])
                for k in range(2)
            ]
            for e in range(1, n_chip)
        ])

    def to_core(d, e, blocks):
        for k in range(2):
            from_core.append(
                remote(blocks[k], part(both[k][1], d, e), pair(core_sem, d, e, k), sibling)
            )

    to_chips(0, (tokens, cotangent))
    firsts = [
        remote(in_a, first_part(0), pair(first_sem, e - 1), chips[e]) for e in range(1, n_chip)
    ]
    to_core(0, 0, (tokens, cotangent))
    from_core.append(remote(in_a, first_part(0), pair(first_core_sem, 0), sibling))
    for d in range(1, n_tok):
        at = pl.multiple_of(((t + d) % n_tok) * width, width)
        depths = pl.ds(pl.multiple_of(t * depth, depth), depth)
        weights.append(remote(
            w_in.at[:, pl.ds(at, width)], full_in.at[depths, :], pair(tok_sem, d - 1, 2), toks[d]
        ))
        weights.append(remote(
            w_out.at[pl.ds(at, width), :], full_out.at[:, depths], pair(tok_sem, d - 1, 3), toks[d]
        ))
    at = pl.multiple_of(t * width, width)
    depths = pl.ds(pl.multiple_of(t * depth, depth), depth)
    own = [
        (tokens, part(x, 0, 0)),
        (cotangent, part(c, 0, 0)),
        (w_in.at[:, pl.ds(at, width)], full_in.at[depths, :]),
        (w_out.at[pl.ds(at, width), :], full_out.at[:, depths]),
        (in_a, first_part(0)),
    ]
    own = [
        pltpu.make_async_copy(source, target, own_sem.at[k])
        for k, (source, target) in enumerate(own)
    ]
    for copy in own:
        copy.start()

    def pass_on(d):
        for e in range(1, n_chip):
            for copy in from_chip[d][e - 1]:
                copy.wait_recv()
            to_core(d, e, (part(x, d, e), part(c, d, e)))

    for d in range(1, n_tok):
        for copy in from_tok[d - 1]:
            copy.wait_recv()
        blocks = (part(x, d, 0), part(c, d, 0))
        to_chips(d, blocks)
        to_core(d, 0, blocks)
        pass_on(d - 1)
    for e in range(1, n_chip):
        firsts[e - 1].wait_recv()
        from_core.append(remote(first_part(e), first_part(e), pair(first_core_sem, e), sibling))
    pass_on(n_tok - 1)
    for copy in from_core + weights:
        copy.wait_recv()
    for copy in own:
        copy.wait()
    for group in from_tok + [firsts, from_core, weights]:
        for copy in group:
            copy.wait_send()
    for groups in from_chip:
        for group in groups:
            for copy in group:
                copy.wait_send()


def gather_inputs(tokens, cotangent, frozen_in, frozen_out, in_a):
    n_tok, n_hid = lax.axis_size("tok"), lax.axis_size("hid")
    n_chip = n_hid // 2
    count, features = tokens.shape[0] * n_tok, tokens.shape[1] * n_hid
    width = frozen_in.shape[1] // n_tok
    sems = pltpu.SemaphoreType.DMA
    vmem = pl.BlockSpec(memory_space=pltpu.VMEM)
    whole = pl.BlockSpec(memory_space=pl.ANY)
    return pl.pallas_call(
        functools.partial(gather_kernel, n_tok, n_hid),
        out_shape=(
            jax.ShapeDtypeStruct((count, features), BF16),
            jax.ShapeDtypeStruct((count, features), BF16),
            jax.ShapeDtypeStruct((features, width), BF16),
            jax.ShapeDtypeStruct((width, features), BF16),
            jax.ShapeDtypeStruct((features, in_a.shape[1]), BF16),
        ),
        in_specs=[vmem] * 5,
        out_specs=(whole,) * 5,
        scratch_shapes=[
            sems((2, n_tok - 1, 4)),
            sems((2, n_tok, n_chip - 1, 2)),
            sems((2, n_tok, n_chip, 2)),
            sems((2, n_chip - 1)),
            sems((2, n_chip)),
            sems((5,)),
        ],
        compiler_params=pltpu.CompilerParams(
            collective_id=2, has_side_effects=True, vmem_limit_bytes=56 * 1024 * 1024
        ),
    )(tokens, cotangent, frozen_in, frozen_out, in_a)


def reduce_kernel(
    n_tok, n_hid, dense, terms, oa, ib,
    dx_out, terms_out, all_oa, all_ib,
    core_d, core_t, send_d, send_t, recv_d, recv_t, kept_d, kept_t, tok_send, tok_recv,
    all_t,
    core_sem, chip_sem, tok_sem, term_sem, grad_sem,
):
    t, h = lax.axis_index("tok"), lax.axis_index("hid")
    n_chip = n_hid // 2
    chip, core = h // 2, h % 2
    rows, cols = dx_out.shape
    count = terms.shape[0]

    def remote(source, target, sems, where):
        return pltpu.make_async_remote_copy(
            src_ref=source, dst_ref=target, send_sem=sems[0], recv_sem=sems[1],
            device_id=where, device_id_type=pl.DeviceIdType.MESH,
        )

    sibling = (t, 2 * chip + 1 - core)
    chips = [(t, 2 * ((chip + e) % n_chip) + core) for e in range(n_chip)]
    toks = [((t + d) % n_tok, h) for d in range(n_tok)]
    barrier = pltpu.get_barrier_semaphore()
    for where in [sibling] + chips[1:] + toks[1:]:
        pl.semaphore_signal(barrier, inc=1, device_id=where, device_id_type=pl.DeviceIdType.MESH)
    pl.semaphore_wait(barrier, n_chip + n_tok - 1)

    def block(index, parity):
        return pl.ds(pl.multiple_of((2 * index + parity) * cols, cols), cols)

    def tok_rows(d):
        return pl.ds(pl.multiple_of(((t + d) % n_tok) * rows, rows), rows)

    chunks = [None] + list(range(1, n_tok)) + [0]
    core_copies, chip_copies, tok_copies = [], [], []
    for q, d in enumerate(chunks):
        group = []
        for e in range(n_chip):
            columns = block((chip + e) % n_chip, 1 - core)
            source = terms.at[:, columns] if d is None else dense.at[tok_rows(d), columns]
            target = core_t.at[e] if d is None else core_d.at[d, e]
            copy = remote(source, target, (core_sem.at[0, q, e], core_sem.at[1, q, e]), sibling)
            copy.start()
            group.append(copy)
        core_copies.append(group)
    grads = ((oa, all_oa), (ib, all_ib))

    def grad_copy(way, k, item):
        at = lax.rem(t + (n_tok - k if way == 0 else k), n_tok)
        to = lax.rem(t + (1 if way == 0 else n_tok - 1), n_tok)
        own, whole = grads[item]
        return remote(
            own if k == 0 else whole.at[at], whole.at[at],
            (grad_sem.at[0, way, k, item], grad_sem.at[1, way, k, item]), (to, h),
        )

    def each_grad(way, k, act):
        for item in range(2):
            act(grad_copy(way, k, item))

    def sends(way, k):
        return jnp.logical_and(t >= k, t < n_tok - 1) if way == 0 else jnp.logical_and(
            t + k < n_tok, t > 0
        )

    def receives(way, k):
        return t >= k + 1 if way == 0 else t + k + 1 < n_tok

    def pass_grads(k):
        for way in range(2):
            if k > 0:
                pl.when(receives(way, k - 1))(
                    lambda way=way: each_grad(way, k - 1, lambda copy: copy.wait_recv())
                )
            if k < n_tok - 1:
                pl.when(sends(way, k))(
                    lambda way=way: each_grad(way, k, lambda copy: copy.start())
                )

    pass_grads(0)

    def over_core(q):
        d, group = chunks[q], []
        for e in range(n_chip):
            core_copies[q][e].wait_recv()
            columns = block((chip + e) % n_chip, core)
            if d is None:
                value = terms[:, columns] + core_t[e]
            else:
                value = dense[tok_rows(d), columns] + core_d[d, e]
            if e == 0:
                if d is None:
                    kept_t[...] = value
                else:
                    kept_d[d] = value
                continue
            sent, got = (send_t, recv_t) if d is None else (send_d.at[d], recv_d.at[d])
            sent[e - 1] = value.astype(BF16)
            copy = remote(
                sent.at[e - 1], got.at[e - 1],
                (chip_sem.at[0, q, e - 1], chip_sem.at[1, q, e - 1]), chips[e],
            )
            copy.start()
            group.append(copy)
        chip_copies.append(group)

    def over_chips(q):
        d = chunks[q]
        for copy in chip_copies[q]:
            copy.wait_recv()
        got = recv_t if d is None else recv_d.at[d]
        value = kept_t[...] if d is None else kept_d[d]
        for e in range(n_chip - 1):
            value = value + got[e].astype(F32)
        if d is None:
            all_t[t] = value.astype(BF16)
            for k in range(1, n_tok):
                copy = remote(
                    all_t.at[t], all_t.at[t], (term_sem.at[0, k - 1], term_sem.at[1, k - 1]), toks[k]
                )
                copy.start()
                tok_copies.append(copy)
        elif d == 0:
            kept_d[0] = value
        else:
            tok_send[d - 1] = value.astype(BF16)
            copy = remote(
                tok_send.at[d - 1], tok_recv.at[d - 1],
                (tok_sem.at[0, d - 1], tok_sem.at[1, d - 1]), toks[d],
            )
            copy.start()
            tok_copies.append(copy)

    over_core(0)
    for q in range(1, n_tok + 1):
        over_core(q)
        over_chips(q - 1)
        if q < n_tok:
            pass_grads(q)
    all_oa[t] = oa[...]
    all_ib[t] = ib[...]
    over_chips(n_tok)
    for copy in tok_copies:
        copy.wait_recv()
    value = all_t[0].astype(F32)
    for k in range(1, n_tok):
        value = value + all_t[k].astype(F32)
    terms_out[...] = value
    value = kept_d[0]
    for d in range(1, n_tok):
        value = value + tok_recv[d - 1].astype(F32)
    dx_out[...] = value
    for group in core_copies + chip_copies + [tok_copies]:
        for copy in group:
            copy.wait_send()
    for k in range(n_tok - 1):
        for way in range(2):
            pl.when(sends(way, k))(
                lambda way=way, k=k: each_grad(way, k, lambda copy: copy.wait_send())
            )


def reduce_outputs(dense, terms, oa, ib):
    n_tok, n_hid = lax.axis_size("tok"), lax.axis_size("hid")
    n_chip = n_hid // 2
    rows, cols = dense.shape[0] // n_tok, dense.shape[1] // n_hid
    count = terms.shape[0]
    width, rank = oa.shape
    sems = pltpu.SemaphoreType.DMA
    vmem = pl.BlockSpec(memory_space=pltpu.VMEM)
    return pl.pallas_call(
        functools.partial(reduce_kernel, n_tok, n_hid),
        out_shape=(
            jax.ShapeDtypeStruct((rows, cols), F32),
            jax.ShapeDtypeStruct((count, cols), F32),
            jax.ShapeDtypeStruct((n_tok, width, rank), BF16),
            jax.ShapeDtypeStruct((n_tok, rank, width), BF16),
        ),
        in_specs=[vmem] * 4,
        out_specs=(vmem,) * 4,
        scratch_shapes=[
            pltpu.VMEM((n_tok, n_chip, rows, cols), F32),
            pltpu.VMEM((n_chip, count, cols), F32),
            pltpu.VMEM((n_tok, n_chip - 1, rows, cols), BF16),
            pltpu.VMEM((n_chip - 1, count, cols), BF16),
            pltpu.VMEM((n_tok, n_chip - 1, rows, cols), BF16),
            pltpu.VMEM((n_chip - 1, count, cols), BF16),
            pltpu.VMEM((n_tok, rows, cols), F32),
            pltpu.VMEM((count, cols), F32),
            pltpu.VMEM((n_tok - 1, rows, cols), BF16),
            pltpu.VMEM((n_tok - 1, rows, cols), BF16),
            pltpu.VMEM((n_tok, count, cols), BF16),
            sems((2, n_tok + 1, n_chip)),
            sems((2, n_tok + 1, n_chip - 1)),
            sems((2, n_tok - 1)),
            sems((2, n_tok - 1)),
            sems((2, 2, n_tok - 1, 2)),
        ],
        compiler_params=pltpu.CompilerParams(
            collective_id=1, has_side_effects=True, vmem_limit_bytes=56 * 1024 * 1024
        ),
    )(dense, terms, oa, ib)


def local(tokens, cotangent, frozen_in, frozen_out, in_a, in_b, out_a, out_b):
    n_tok, t = lax.axis_size("tok"), lax.axis_index("tok")
    rank = in_b.shape[0]
    count = tokens.shape[0] * n_tok
    scale = ADAPTER_SCALE / math.sqrt(count)
    width = frozen_in.shape[1] // n_tok
    x, c, w_in, w_out, in_a_full = gather_inputs(tokens, cotangent, frozen_in, frozen_out, in_a)
    second = lax.dynamic_slice_in_dim(in_b, t * width, width, 1)
    first = lax.dynamic_slice_in_dim(out_a, t * width, width, 0)
    half_second = (ADAPTER_SCALE * second).astype(BF16)
    half_first = (ADAPTER_SCALE * first).astype(BF16)
    half_in_a = (ADAPTER_SCALE * in_a_full).astype(BF16)
    low_in = halves(dot(x, in_a_full, ((1,), (0,))))
    back_low = halves(dot(c, out_b, ((1,), (1,))))
    pre = dot(x, w_in, ((1,), (0,))) + dot(
        low_in, jnp.concatenate([half_second, half_second], axis=0), ((1,), (0,))
    )
    value_out, slopes = gelu_pair(pre)
    act = value_out.astype(BF16)
    dense_back = dot(c, w_out, ((1,), (1,))) + dot(
        back_low, jnp.concatenate([half_first, half_first], axis=1), ((1,), (1,))
    )
    grad_pre = (dense_back * slopes).astype(BF16)
    oa = dot(act, back_low, ((0,), (0,)))
    oa = scale * (oa[:, :rank] + oa[:, rank:])
    ib = dot(low_in, grad_pre, ((0,), (0,)))
    ib = scale * (ib[:rank] + ib[rank:])
    rank_out = halves(dot(act, first, ((1,), (0,))))
    rank_back = halves(dot(grad_pre, second, ((1,), (1,))))
    dense = dot(grad_pre, w_in, ((1,), (1,))) + dot(
        rank_back, jnp.concatenate([half_in_a, half_in_a], axis=1), ((1,), (1,))
    )
    out_term = dot(rank_out, c, ((0,), (0,)))
    in_term = dot(rank_back, x, ((0,), (0,)))
    terms = scale * jnp.concatenate(
        [out_term[:rank] + out_term[rank:], in_term[:rank] + in_term[rank:]], axis=0
    )
    input_gradient, total, grad_out_a, grad_in_b = reduce_outputs(
        dense, terms, oa.astype(BF16), ib.astype(BF16)
    )
    grad_out_a = grad_out_a.reshape(-1, rank).astype(F32)
    grad_in_b = grad_in_b.transpose(1, 0, 2).reshape(rank, -1).astype(F32)
    return (input_gradient, total[rank:].T, grad_in_b, grad_out_a, total[:rank])


def local_by_rows(
    tokens,
    cotangent,
    frozen_in,
    frozen_out,
    input_adapter_first,
    input_adapter_second,
    adapter_out_a,
    adapter_out_b,
):
    highest_precision = lax.Precision.HIGHEST
    device_local_rows = tokens.shape[0]
    rank_width = input_adapter_second.shape[0]
    gradient_scale = ADAPTER_SCALE / math.sqrt(device_local_rows * lax.axis_size("tok"))
    full_tokens, full_cotan = (
        lax.all_gather(tokens, "hid", axis=1, tiled=True),
        lax.all_gather(cotangent, "hid", axis=1, tiled=True),
    )
    in_rows = lax.all_gather(frozen_in, "tok", axis=0, tiled=True)
    in_a_full = lax.all_gather(input_adapter_first, "hid", axis=0, tiled=True)
    lowrank_input = jnp.dot(full_tokens, in_a_full, preferred_element_type=jnp.float32)
    second_float = input_adapter_second.astype(jnp.float32)
    out_a_float = adapter_out_a.astype(jnp.float32)
    pre_activation = jnp.dot(
        full_tokens, in_rows, preferred_element_type=jnp.float32
    ) + ADAPTER_SCALE * jnp.dot(lowrank_input, second_float, precision=highest_precision)
    value_out, slopes = gelu_pair(pre_activation)
    hidden_act = value_out.astype(jnp.bfloat16)
    backward_lowrank = jnp.einsum(
        "td,rd->tr", full_cotan, adapter_out_b, preferred_element_type=jnp.float32
    )
    rank_out = jnp.dot(hidden_act, adapter_out_a, preferred_element_type=jnp.float32)
    dense_backward = jnp.einsum(
        "td,fd->tf",
        full_cotan,
        lax.all_gather(frozen_out, "tok", axis=1, tiled=True),
        preferred_element_type=jnp.float32,
    )
    dense_backward = dense_backward + ADAPTER_SCALE * jnp.dot(
        backward_lowrank, out_a_float.T, precision=highest_precision
    )
    grad_pre = (dense_backward * slopes).astype(jnp.bfloat16)
    rank_backward = jnp.einsum(
        "tf,rf->tr", grad_pre, input_adapter_second, preferred_element_type=jnp.float32
    )
    dense_in = jnp.einsum("tf,df->td", grad_pre, in_rows, preferred_element_type=jnp.float32)
    grad_out_a = gradient_scale * jnp.dot(
        hidden_act.astype(jnp.float32).T, backward_lowrank, precision=highest_precision
    )
    grad_in_b = gradient_scale * jnp.dot(
        lowrank_input.T, grad_pre.astype(jnp.float32), precision=highest_precision
    )
    in_a_float = in_a_full.astype(jnp.float32)
    dx_term = dense_in + ADAPTER_SCALE * jnp.dot(
        rank_backward, in_a_float.T, precision=highest_precision
    )
    out_term = jnp.dot(rank_out.T, full_cotan.astype(jnp.float32), precision=highest_precision)
    in_term = jnp.dot(rank_backward.T, full_tokens.astype(jnp.float32), precision=highest_precision)
    rank_terms = jnp.concatenate([out_term, in_term], axis=0)
    input_gradient, rank_local = (
        lax.psum_scatter(dx_term, "hid", scatter_dimension=1, tiled=True),
        lax.psum_scatter(rank_terms, "hid", scatter_dimension=1, tiled=True),
    )
    grad_out_a, grad_in_b, rank_total = lax.psum((grad_out_a, grad_in_b, rank_local), "tok")
    grad_out_b = gradient_scale * rank_total[:rank_width]
    grad_in_a = gradient_scale * rank_total[rank_width:].T
    return (input_gradient, grad_in_a, grad_in_b, grad_out_a, grad_out_b)


def solution(mesh):
    in_specs = (
        P("tok", "hid"),
        P("tok", "hid"),
        P("tok", "hid"),
        P("hid", "tok"),
        P("hid", None),
        P(None, "hid"),
        P("hid", None),
        P(),
    )
    out_specs = (P("tok", "hid"), P("hid", None), P(None, "hid"), P("hid", None), P(None, "hid"))
    def body(*arrays):
        share = arrays[2].shape[1] // lax.axis_size("tok")
        return local(*arrays) if share % 128 == 0 else local_by_rows(*arrays)

    return jax.shard_map(body, mesh=mesh, in_specs=in_specs, out_specs=out_specs, check_vma=False)
```
